32 devices in a mesh: groups: 2 (over x), row: 16 (over z, y, core).
Axes of the slice: x: 2, y: 2, z: 4, core: 2. Of those that a mesh axis runs over, the one named last changes fastest.
Arguments:
- inputs: bfloat16 [1024, 8192], P(('groups', 'row')), parts along dimension 0, may hold values from -6 to 6
- input_factor: bfloat16 [16384, 8192], P(('groups', 'row')), parts along dimension 0, as said below
- out_grads: bfloat16 [1024, 16384], P(('groups', 'row')), parts along dimension 0, may hold values from -6 to 6
- output_factor: float32 [32768, 4096], P(('groups', 'row')), parts along dimension 0, may hold values from -6 to 6
Outputs:
- updated_factor: float32 [32768, 4096], P(('groups', 'row')), parts along dimension 0
The draws below stay inside these ranges and needn't reach their ends.
There are 2 independent parts, one for each index of `groups`. The reference program is written for one: setup_inputs(seed, part) draws one part's arguments, and reference() takes and returns one part's arrays. A program takes and returns all parts, laid end to end along the dimension named above; each array names one. Nothing has to cross between parts.
Inputs may be any that keep to these rules, and one draw needn't show every extreme that they name: input_factor is symmetric.
All inputs are finite; a program needn't handle non-finite values.
Results may differ from the reference program's by a relative error of at most 0.0041.
Values may be sent and summed in bfloat16 or wider, within the bound.
A program may use at most 192 MiB of HBM per device.

```python
import jax
import jax.numpy as jnp

DIN = 8192
DOUT = 16384
SLAB = 4096
TOKENS = 512
N_ROW = 16


def draw_input_factor(key, part):
    base = jax.random.truncated_normal(key, -4.0, 4.0, (DIN, DIN), jnp.float32)
    symmetric = (base + base.T) * 0.5 ** 0.5
    width = DIN // N_ROW
    row_block = jnp.arange(DIN, dtype=jnp.int32) // width
    same_block = (row_block[:, None] == row_block[None, :]).astype(jnp.float32)
    boosted = symmetric * (1.0 + 2.0 * same_block)
    return (boosted * float(DIN) ** (-0.5)).astype(jnp.bfloat16)


def block_scale(key, shape, split, low, high):
    def one(position, parts):
        draws = jax.random.uniform(jax.random.fold_in(jax.random.fold_in(key, 6), position), (parts,), jnp.float32, low / len(split), high / len(split))
        return jnp.repeat(jnp.exp(draws), shape[position] // parts).reshape((-1,) + (1,) * (len(shape) - position - 1))

    factor_of = one(*split[0])
    for cut in split[1:]:
        factor_of = factor_of * one(*cut)
    return factor_of


def scatter_about(rng, dims, scale, reach, cuts=(), kind=jnp.bfloat16):
    level = block_scale(rng, dims, cuts, -0.22, 0.18) if cuts else 1.0
    values = jax.random.normal(rng, dims, jnp.float32) * scale * level
    return jnp.minimum(jnp.maximum(values, -reach), reach).astype(kind)


def setup_inputs(seed: int = 0, part: int = 0) -> dict:
    splits = jax.random.split(jax.random.key(seed), 5)
    own_keys = jax.random.split(jax.random.fold_in(splits[4], part), 5)
    return {
        "inputs": scatter_about(own_keys[0], (TOKENS, DIN), 1.0, 6.0, ((0, 16),)),
        "input_factor": draw_input_factor(jax.random.fold_in(jax.random.fold_in(splits[4], part), 71), part),
        "out_grads": scatter_about(own_keys[2], (TOKENS, DOUT), 1.0, 6.0, ((0, 16),)),
        "output_factor": scatter_about(own_keys[3], (DOUT, SLAB), 1.0, 6.0, ((0, 16),), jnp.float32),
    }


def reference(inputs, input_factor, out_grads, output_factor):
    projected = jnp.dot(inputs, input_factor, preferred_element_type=jnp.float32).astype(jnp.bfloat16)
    summed = jnp.dot(projected, inputs.T, preferred_element_type=jnp.float32)
    gram = (summed * (float(DIN) ** -0.5)).astype(jnp.bfloat16)
    left = jnp.dot(out_grads.T, gram, preferred_element_type=jnp.float32).astype(jnp.bfloat16)
    update = jnp.dot(left, out_grads[:, :SLAB], preferred_element_type=jnp.float32)
    return output_factor + update * (1.0 / TOKENS)
```

```python
import functools

import jax
import jax.numpy as jnp
from jax import lax
from jax.experimental import pallas as pl
from jax.experimental.pallas import tpu as pltpu
from jax.sharding import PartitionSpec as P

UP, DOWN, SIDE, CORE = range(4)


def exchange_kernel(
    n, x_ref, f_ref, g_ref, gram_ref, slab_ref, cols_ref,
    xall, fv, gv, proj, part, out0, in0, out1, in1, out2, in2, final,
    local_sem, x_recv, x_send, s_recv, s_send, c_recv, c_send,
    r_recv, r_send, z2_recv, z2_send, z3_recv, z3_send,
):
    me = lax.axis_index("row")
    depth = n // 4
    z, y, c = me // 4, (me // 2) % 2, me % 2
    sh = x_ref.shape[0]
    tokens = n * sh
    slab = slab_ref.shape[1]
    width = cols_ref.shape[1]
    feat = f_ref.shape[0]

    def index(zz, yy, cc):
        return zz * 4 + yy * 2 + cc

    side, peer = index(z, 1 - y, c), index(z, y, 1 - c)

    def rows(start, size):
        return pl.ds(pl.multiple_of(start, size), size)

    load_f = pltpu.make_async_copy(f_ref, fv, local_sem.at[0])
    load_x = pltpu.make_async_copy(x_ref, xall.at[rows(me * sh, sh), :], local_sem.at[1])
    load_g = pltpu.make_async_copy(g_ref, gv, local_sem.at[2])
    load_x.start()
    load_g.start()
    load_f.start()

    barrier = pltpu.get_barrier_semaphore()
    for k in range(1, n):
        pl.semaphore_signal(
            barrier, inc=1, device_id={"row": (me + k) % n}, device_id_type=pl.DeviceIdType.MESH
        )
    pl.semaphore_wait(barrier, n - 1)

    def send(src, dst, send_sem, recv_sem, target):
        return pltpu.make_async_remote_copy(
            src_ref=src, dst_ref=dst, send_sem=send_sem, recv_sem=recv_sem,
            device_id={"row": target}, device_id_type=pl.DeviceIdType.MESH,
        )

    class Gather:
        def __init__(self, buf, recv, sems):
            self.buf, self.recv, self.sems = buf, recv, sems

        def copy(self, origin, kind, target, src=None):
            view = self.buf.at[rows(origin * sh, sh), :]
            return send(
                view if src is None else src, view,
                self.sems.at[kind, origin], self.recv.at[origin], target,
            )

        def arrived(self, origin):
            self.copy(origin, CORE, peer).wait_recv()

        def own(self, src):
            @pl.when(z + 1 < depth)
            def _():
                self.copy(me, UP, index(z + 1, y, c), src).start()

            @pl.when(z > 0)
            def _():
                self.copy(me, DOWN, index(z - 1, y, c), src).start()

            self.copy(me, SIDE, side, src).start()
            self.copy(me, CORE, peer, src).start()

        def column(self, k):
            @pl.when(z - k >= 0)
            def _():
                origin = index(z - k, y, c)
                self.arrived(origin)

                @pl.when(z + 1 < depth)
                def _():
                    self.copy(origin, UP, index(z + 1, y, c)).start()

                self.copy(origin, SIDE, side).start()
                self.copy(origin, CORE, peer).start()

            @pl.when(z + k < depth)
            def _():
                origin = index(z + k, y, c)
                self.arrived(origin)

                @pl.when(z > 0)
                def _():
                    self.copy(origin, DOWN, index(z - 1, y, c)).start()

                self.copy(origin, SIDE, side).start()
                self.copy(origin, CORE, peer).start()

        def across(self, plane):
            origin = index(plane, 1 - y, c)
            self.arrived(origin)
            self.copy(origin, CORE, peer).start()

        def whole(self, plane):
            self.arrived(index(plane, 0, 1 - c))
            self.arrived(index(plane, 1, 1 - c))

        def drain(self):
            for plane in range(depth):
                origin = index(plane, y, c)

                @pl.when((plane <= z) & (z + 1 < depth))
                def _():
                    self.copy(origin, UP, side).wait_send()

                @pl.when((plane >= z) & (z > 0))
                def _():
                    self.copy(origin, DOWN, side).wait_send()

                self.copy(origin, SIDE, side).wait_send()
                self.copy(origin, CORE, peer).wait_send()
                self.copy(index(plane, 1 - y, c), CORE, peer).wait_send()

    gx = Gather(xall, x_recv, x_send)
    gs = Gather(slab_ref, s_recv, s_send)
    gx.own(x_ref)

    flip = z >= (depth + 1) // 2
    zm = jnp.where(flip, depth - 1 - z, z)

    def plane_at(t):
        near = zm - (t + 1) // 2 if t % 2 else zm + t // 2
        p = jnp.where(t <= 2 * zm, near, t)
        return jnp.where(flip, depth - 1 - p, p)

    block = 4 * sh
    tile = min(256, feat)

    def project(plane):
        xs = rows(plane * block, block)

        @pl.loop(0, feat // tile)
        def _(j):
            fs = rows(j * tile, tile)
            proj[xs, fs] = lax.dot_general(
                xall[xs, :], fv[fs, :], (((1,), (1,)), ((), ())),
                preferred_element_type=jnp.float32,
            ).astype(jnp.bfloat16)

    def cols_copy(d, origin):
        return send(
            gv.at[:, rows(d * width, width)],
            cols_ref.at[rows(origin * sh, sh), :],
            c_send.at[d], c_recv.at[origin], d,
        )

    load_x.wait()
    load_g.wait()
    load_f.wait()
    own_slab = pltpu.make_async_copy(
        gv.at[:, pl.ds(0, slab)], slab_ref.at[rows(me * sh, sh), :], local_sem.at[3]
    )
    own_cols = pltpu.make_async_copy(
        gv.at[:, rows(me * width, width)], cols_ref.at[rows(me * sh, sh), :], local_sem.at[4]
    )
    own_slab.start()
    own_cols.start()

    for t in range(depth):
        if t > 0:
            gx.column(t)
        if t == depth - 1:
            gs.own(gv.at[:, pl.ds(0, slab)])
            for k in range(1, n):
                cols_copy((me + k) % n, me).start()
        plane = plane_at(t)
        gx.across(plane)
        gx.whole(plane)
        project(plane)

    own_features = rows(me * feat, feat)
    half, quarter = tokens // 2, tokens // 4

    def partial_rows(start, size):
        return lax.dot_general(
            proj[rows(start, size), :], xall[:, own_features], (((1,), (1,)), ((), ())),
            preferred_element_type=jnp.float32,
        )

    out0[...] = partial_rows((1 - c) * half, half).astype(jnp.bfloat16)
    core_sum = send(out0, in0, r_send.at[0], r_recv.at[0], peer)
    core_sum.start()
    part[...] = partial_rows(c * half, half)
    if depth > 1:
        gs.column(1)
    core_sum.wait_recv()
    gone, kept = rows((1 - y) * quarter, quarter), rows(y * quarter, quarter)
    out1[...] = (part[gone, :] + in0[gone, :].astype(jnp.float32)).astype(jnp.bfloat16)
    side_sum = send(out1, in1, r_send.at[1], r_recv.at[1], side)
    side_sum.start()
    part[kept, :] = part[kept, :] + in0[kept, :].astype(jnp.float32)
    if depth > 2:
        gs.column(2)
    side_sum.wait_recv()
    part[kept, :] = part[kept, :] + in1[...].astype(jnp.float32)
    out2[...] = part[kept, :].astype(jnp.bfloat16)

    def z_sum(k):
        zz = (z + k) % depth
        return send(
            out2.at[rows(zz * sh, sh), :], in2.at[k], z2_send.at[k], z2_recv.at[k], index(zz, y, c)
        )

    for k in range(1, depth):
        z_sum(k).start()
    total = part[rows(y * quarter + z * sh, sh), :]
    for k in range(1, depth):
        z_sum(k).wait_recv()
        total = total + in2[k].astype(jnp.float32)
    scale = float(n * feat) ** (-0.5)
    base = c * half + y * quarter
    mine = rows(base + z * sh, sh)
    final[mine, :] = (total * scale).astype(jnp.bfloat16)

    def z_spread(k):
        zz = (z + k) % depth
        return send(
            final.at[mine, :], final.at[mine, :], z3_send.at[k], z3_recv.at[k], index(zz, y, c)
        )

    for k in range(1, depth):
        z_spread(k).start()
    for k in range(3, depth):
        gs.column(k)
    for k in range(1, depth):
        z_spread(k).wait_recv()
    view = final.at[rows(base, quarter), :]
    side_spread = send(view, view, r_send.at[2], r_recv.at[2], side)
    side_spread.start()
    side_spread.wait_recv()
    view = final.at[rows(c * half, half), :]
    core_spread = send(view, view, r_send.at[3], r_recv.at[3], peer)
    core_spread.start()
    for t in range(depth):
        gs.across(plane_at(t))
    core_spread.wait_recv()
    gram_ref[...] = final[...]
    for t in range(depth):
        gs.whole(plane_at(t))
    for k in range(1, n):
        cols_copy(me, (me + k) % n).wait_recv()

    gx.drain()
    gs.drain()
    for k in range(1, n):
        cols_copy((me + k) % n, me).wait_send()
    for copy in (core_sum, side_sum, side_spread, core_spread):
        copy.wait_send()
    for k in range(1, depth):
        z_sum(k).wait_send()
        z_spread(k).wait_send()
    own_slab.wait()
    own_cols.wait()


def exchange(n, x, f, g, slab):
    sh, din = x.shape
    feat = f.shape[0]
    tokens, depth = n * sh, n // 4
    width = g.shape[1] // n
    half, quarter = tokens // 2, tokens // 4
    bf, dma = jnp.bfloat16, pltpu.SemaphoreType.DMA
    anyspace = pl.BlockSpec(memory_space=pl.ANY)
    return pl.pallas_call(
        functools.partial(exchange_kernel, n),
        out_shape=(
            jax.ShapeDtypeStruct((tokens, tokens), bf),
            jax.ShapeDtypeStruct((tokens, slab), bf),
            jax.ShapeDtypeStruct((tokens, width), bf),
        ),
        in_specs=[anyspace] * 3,
        out_specs=(pl.BlockSpec(memory_space=pltpu.VMEM), anyspace, anyspace),
        scratch_shapes=[
            pltpu.VMEM((tokens, din), bf),
            pltpu.VMEM(f.shape, bf),
            pltpu.VMEM(g.shape, bf),
            pltpu.VMEM((tokens, feat), bf),
            pltpu.VMEM((half, tokens), jnp.float32),
            pltpu.VMEM((half, tokens), bf),
            pltpu.VMEM((half, tokens), bf),
            pltpu.VMEM((quarter, tokens), bf),
            pltpu.VMEM((quarter, tokens), bf),
            pltpu.VMEM((quarter, tokens), bf),
            pltpu.VMEM((depth, sh, tokens), bf),
            pltpu.VMEM((tokens, tokens), bf),
            dma((5,)), dma((n,)), dma((4, n)), dma((n,)), dma((4, n)),
            dma((n,)), dma((n,)), dma((4,)), dma((4,)),
            dma((depth,)), dma((depth,)), dma((depth,)), dma((depth,)),
        ],
        compiler_params=pltpu.CompilerParams(
            collective_id=0, has_side_effects=True, vmem_limit_bytes=60 * 1024 * 1024
        ),
    )(x, f, g)


def per_device(n, inputs, input_factor, out_grads, output_factor):
    slab_width = output_factor.shape[1]
    gram, slab_all, grad_cols = exchange(n, inputs, input_factor, out_grads, slab_width)
    left = lax.dot_general(
        grad_cols, gram, (((0,), (0,)), ((), ())), preferred_element_type=jnp.float32
    ).astype(jnp.bfloat16)
    update = jnp.dot(left, slab_all, preferred_element_type=jnp.float32)
    return output_factor + update * (1.0 / gram.shape[0])


def solution(mesh):
    spec = P(("groups", "row"), None)
    return jax.shard_map(
        functools.partial(per_device, mesh.shape["row"]),
        mesh=mesh, in_specs=(spec,) * 4, out_specs=spec, check_vma=False,
    )
```

```python
import functools

import jax
import jax.numpy as jnp
from jax import lax
from jax.experimental import pallas as pl
from jax.experimental.pallas import tpu as pltpu
from jax.sharding import PartitionSpec as P

UP, DOWN, SIDE, CORE = range(4)


def exchange_kernel(
    n, x_ref, f_ref, g_ref, gram_ref, slab_ref, cols_ref,
    xall, fv, gv, proj, proj_low, part, out0, in0, out1, in1, out2, in2, final,
    local_sem, x_recv, x_send, s_recv, s_send, c_recv, c_send,
    r_recv, r_send, z2_recv, z2_send, z3_recv, z3_send,
):
    me = lax.axis_index("row")
    depth = n // 4
    z, y, c = me // 4, (me // 2) % 2, me % 2
    sh = x_ref.shape[0]
    tokens = n * sh
    slab = slab_ref.shape[1]
    width = cols_ref.shape[1]
    feat = f_ref.shape[0]

    def index(zz, yy, cc):
        return zz * 4 + yy * 2 + cc

    side, peer = index(z, 1 - y, c), index(z, y, 1 - c)

    def rows(start, size):
        return pl.ds(pl.multiple_of(start, size), size)

    load_f = pltpu.make_async_copy(f_ref, fv, local_sem.at[0])
    load_x = pltpu.make_async_copy(x_ref, xall.at[rows(me * sh, sh), :], local_sem.at[1])
    load_g = pltpu.make_async_copy(g_ref, gv, local_sem.at[2])
    load_x.start()
    load_g.start()
    load_f.start()

    barrier = pltpu.get_barrier_semaphore()
    for k in range(1, n):
        pl.semaphore_signal(
            barrier, inc=1, device_id={"row": (me + k) % n}, device_id_type=pl.DeviceIdType.MESH
        )
    pl.semaphore_wait(barrier, n - 1)

    def send(src, dst, send_sem, recv_sem, target):
        return pltpu.make_async_remote_copy(
            src_ref=src, dst_ref=dst, send_sem=send_sem, recv_sem=recv_sem,
            device_id={"row": target}, device_id_type=pl.DeviceIdType.MESH,
        )

    chips = n // 2
    chip = z * 2 + y
    window = min(chips, chips // 2 + 1)
    union = min(chips, window + 1)

    class Gather:
        def __init__(self, buf, recv, sems, pieces):
            self.buf, self.recv, self.sems, self.pieces = buf, recv, sems, pieces
            self.width = buf.shape[1] // pieces
            self.near = window if pieces > 1 else 1
            self.end = union if pieces > 1 else 1

        def copy(self, origin, kind, target, first, count, src=None):
            cols = pl.ds(pl.multiple_of(first * self.width, self.width), count * self.width)
            view = self.buf.at[rows(origin * sh, sh), cols]
            return send(
                view if src is None else src.at[:, cols], view,
                self.sems.at[kind, origin], self.recv.at[origin], target,
            )

        def start(self, origin, kind, target, first, count, src=None):
            if self.pieces == 1:
                self.copy(origin, kind, target, 0, 1, src).start()
                return

            @pl.loop(0, count)
            def _(k):
                self.copy(origin, kind, target, (first + k) % self.pieces, 1, src).start()

        def along(self, origin, kind, src=None):
            to = z + 1 if kind == UP else z - 1
            last = (to == depth - 1) | (to == 0)
            count = jnp.where(last, self.end, self.pieces)
            self.start(origin, kind, index(to, y, c), to * 2, count, src)

        def near_by(self, origin, src=None):
            self.start(origin, SIDE, side, z * 2 + 1 - y, self.near, src)
            self.start(origin, CORE, peer, chip, self.near, src)

        def arrived(self, origin, count):
            self.copy(origin, CORE, peer, 0, count).wait_recv()

        def own(self, src):
            @pl.when(z + 1 < depth)
            def _():
                self.along(me, UP, src)

            @pl.when(z > 0)
            def _():
                self.along(me, DOWN, src)

            self.near_by(me, src)

        def column(self, k):
            def came(origin):
                last = (z == depth - 1) | (z == 0)

                @pl.when(last)
                def _():
                    self.arrived(origin, self.end)

                @pl.when(jnp.logical_not(last))
                def _():
                    self.arrived(origin, self.pieces)

            @pl.when(z - k >= 0)
            def _():
                origin = index(z - k, y, c)
                came(origin)

                @pl.when(z + 1 < depth)
                def _():
                    self.along(origin, UP)

                self.near_by(origin)

            @pl.when(z + k < depth)
            def _():
                origin = index(z + k, y, c)
                came(origin)

                @pl.when(z > 0)
                def _():
                    self.along(origin, DOWN)

                self.near_by(origin)

        def across(self, plane):
            origin = index(plane, 1 - y, c)
            self.arrived(origin, self.near)
            self.start(origin, CORE, peer, chip, self.near)

        def whole(self, plane):
            self.arrived(index(plane, 0, 1 - c), self.near)
            self.arrived(index(plane, 1, 1 - c), self.near)

        def drain(self):
            def sent(origin, kind, count):
                self.copy(origin, kind, peer, 0, count).wait_send()

            for plane in range(depth):
                origin = index(plane, y, c)
                for kind, edge, gate in (
                    (UP, z + 1 == depth - 1, (plane <= z) & (z + 1 < depth)),
                    (DOWN, z - 1 == 0, (plane >= z) & (z > 0)),
                ):
                    @pl.when(gate & edge)
                    def _():
                        sent(origin, kind, self.end)

                    @pl.when(gate & jnp.logical_not(edge))
                    def _():
                        sent(origin, kind, self.pieces)

                sent(origin, SIDE, self.near)
                sent(origin, CORE, self.near)
                sent(index(plane, 1 - y, c), CORE, self.near)

    gx = Gather(xall, x_recv, x_send, chips)
    gs = Gather(slab_ref, s_recv, s_send, 1)
    gx.own(x_ref)

    flip = z >= (depth + 1) // 2
    zm = jnp.where(flip, depth - 1 - z, z)

    def plane_at(t):
        near = zm - (t + 1) // 2 if t % 2 else zm + t // 2
        p = jnp.where(t <= 2 * zm, near, t)
        return jnp.where(flip, depth - 1 - p, p)

    block = 4 * sh
    tile = min(256, feat)

    def project(plane):
        xs = rows(plane * block, block)

        @pl.loop(0, feat // tile)
        def _(j):
            fs = rows(j * tile, tile)
            edge, inner = jnp.zeros((block, tile), jnp.float32), jnp.zeros((block, tile), jnp.float32)
            for k in range(window):
                cs = rows((chip + k) % chips * (2 * feat), 2 * feat)
                term = lax.dot_general(
                    xall[xs, cs], fv[fs, cs], (((1,), (1,)), ((), ())),
                    preferred_element_type=jnp.float32,
                )
                if k == 0 or 2 * k == chips:
                    edge = edge + term
                else:
                    inner = inner + term
            value = inner + 0.5 * edge
            high = value.astype(jnp.bfloat16)
            proj[xs, fs] = high
            proj_low[xs, fs] = (value - high.astype(jnp.float32)).astype(jnp.bfloat16)

    def cols_copy(d, origin):
        return send(
            gv.at[:, rows(d * width, width)],
            cols_ref.at[rows(origin * sh, sh), :],
            c_send.at[d], c_recv.at[origin], d,
        )

    load_x.wait()
    load_g.wait()
    load_f.wait()
    own_slab = pltpu.make_async_copy(
        gv.at[:, pl.ds(0, slab)], slab_ref.at[rows(me * sh, sh), :], local_sem.at[3]
    )
    own_cols = pltpu.make_async_copy(
        gv.at[:, rows(me * width, width)], cols_ref.at[rows(me * sh, sh), :], local_sem.at[4]
    )
    own_slab.start()
    own_cols.start()

    for t in range(depth):
        if t > 0:
            gx.column(t)
        if t == depth - 1:
            gs.own(gv.at[:, pl.ds(0, slab)])
            for k in range(1, n):
                cols_copy((me + k) % n, me).start()
        plane = plane_at(t)
        gx.across(plane)
        gx.whole(plane)
        project(plane)

    own_features = rows(me * feat, feat)
    half, quarter = tokens // 2, tokens // 4

    def partial_rows(start, size):
        some = rows(start, size)
        total = jnp.zeros((size, tokens), jnp.float32)
        for piece in (proj, proj_low):
            for left, right in ((piece[some, :], xall[:, own_features]), (xall[some, own_features], piece[...])):
                total = total + lax.dot_general(
                    left, right, (((1,), (1,)), ((), ())), preferred_element_type=jnp.float32
                )
        return total

    out0[...] = partial_rows((1 - c) * half, half)
    core_sum = send(out0, in0, r_send.at[0], r_recv.at[0], peer)
    core_sum.start()
    part[...] = partial_rows(c * half, half)
    if depth > 1:
        gs.column(1)
    core_sum.wait_recv()
    gone, kept = rows((1 - y) * quarter, quarter), rows(y * quarter, quarter)
    out1[...] = (part[gone, :] + in0[gone, :]).astype(jnp.bfloat16)
    side_sum = send(out1, in1, r_send.at[1], r_recv.at[1], side)
    side_sum.start()
    part[kept, :] = part[kept, :] + in0[kept, :]
    if depth > 2:
        gs.column(2)
    side_sum.wait_recv()
    part[kept, :] = part[kept, :] + in1[...].astype(jnp.float32)
    out2[...] = part[kept, :].astype(jnp.bfloat16)

    def z_sum(k):
        zz = (z + k) % depth
        return send(
            out2.at[rows(zz * sh, sh), :], in2.at[k], z2_send.at[k], z2_recv.at[k], index(zz, y, c)
        )

    for k in range(1, depth):
        z_sum(k).start()
    total = part[rows(y * quarter + z * sh, sh), :]
    for k in range(1, depth):
        z_sum(k).wait_recv()
        total = total + in2[k].astype(jnp.float32)
    scale = float(n * feat) ** (-0.5)
    base = c * half + y * quarter
    mine = rows(base + z * sh, sh)
    final[mine, :] = (total * scale).astype(jnp.bfloat16)

    def z_spread(k):
        zz = (z + k) % depth
        return send(
            final.at[mine, :], final.at[mine, :], z3_send.at[k], z3_recv.at[k], index(zz, y, c)
        )

    for k in range(1, depth):
        z_spread(k).start()
    for k in range(3, depth):
        gs.column(k)
    for k in range(1, depth):
        z_spread(k).wait_recv()
    view = final.at[rows(base, quarter), :]
    side_spread = send(view, view, r_send.at[2], r_recv.at[2], side)
    side_spread.start()
    side_spread.wait_recv()
    view = final.at[rows(c * half, half), :]
    core_spread = send(view, view, r_send.at[3], r_recv.at[3], peer)
    core_spread.start()
    for t in range(depth):
        gs.across(plane_at(t))
    core_spread.wait_recv()
    gram_ref[...] = final[...]
    for t in range(depth):
        gs.whole(plane_at(t))
    for k in range(1, n):
        cols_copy(me, (me + k) % n).wait_recv()

    gx.drain()
    gs.drain()
    for k in range(1, n):
        cols_copy((me + k) % n, me).wait_send()
    for copy in (core_sum, side_sum, side_spread, core_spread):
        copy.wait_send()
    for k in range(1, depth):
        z_sum(k).wait_send()
        z_spread(k).wait_send()
    own_slab.wait()
    own_cols.wait()


def exchange(n, x, f, g, slab):
    sh, din = x.shape
    feat = f.shape[0]
    tokens, depth = n * sh, n // 4
    width = g.shape[1] // n
    half, quarter = tokens // 2, tokens // 4
    bf, dma = jnp.bfloat16, pltpu.SemaphoreType.DMA
    anyspace = pl.BlockSpec(memory_space=pl.ANY)
    return pl.pallas_call(
        functools.partial(exchange_kernel, n),
        out_shape=(
            jax.ShapeDtypeStruct((tokens, tokens), bf),
            jax.ShapeDtypeStruct((tokens, slab), bf),
            jax.ShapeDtypeStruct((tokens, width), bf),
        ),
        in_specs=[anyspace] * 3,
        out_specs=(pl.BlockSpec(memory_space=pltpu.VMEM), anyspace, anyspace),
        scratch_shapes=[
            pltpu.VMEM((tokens, din), bf),
            pltpu.VMEM(f.shape, bf),
            pltpu.VMEM(g.shape, bf),
            pltpu.VMEM((tokens, feat), bf),
            pltpu.VMEM((tokens, feat), bf),
            pltpu.VMEM((half, tokens), jnp.float32),
            pltpu.VMEM((half, tokens), jnp.float32),
            pltpu.VMEM((half, tokens), jnp.float32),
            pltpu.VMEM((quarter, tokens), bf),
            pltpu.VMEM((quarter, tokens), bf),
            pltpu.VMEM((quarter, tokens), bf),
            pltpu.VMEM((depth, sh, tokens), bf),
            pltpu.VMEM((tokens, tokens), bf),
            dma((5,)), dma((n,)), dma((4, n)), dma((n,)), dma((4, n)),
            dma((n,)), dma((n,)), dma((4,)), dma((4,)),
            dma((depth,)), dma((depth,)), dma((depth,)), dma((depth,)),
        ],
        compiler_params=pltpu.CompilerParams(
            collective_id=0, has_side_effects=True, vmem_limit_bytes=60 * 1024 * 1024
        ),
    )(x, f, g)


def per_device(n, inputs, input_factor, out_grads, output_factor):
    slab_width = output_factor.shape[1]
    gram, slab_all, grad_cols = exchange(n, inputs, input_factor, out_grads, slab_width)
    left = lax.dot_general(
        grad_cols, gram, (((0,), (0,)), ((), ())), preferred_element_type=jnp.float32
    ).astype(jnp.bfloat16)
    update = jnp.dot(left, slab_all, preferred_element_type=jnp.float32)
    return output_factor + update * (1.0 / gram.shape[0])


def solution(mesh):
    spec = P(("groups", "row"), None)
    return jax.shard_map(
        functools.partial(per_device, mesh.shape["row"]),
        mesh=mesh, in_specs=(spec,) * 4, out_specs=spec, check_vma=False,
    )
```

```python
import functools

import jax
import jax.numpy as jnp
from jax import lax
from jax.experimental import pallas as pl
from jax.experimental.pallas import tpu as pltpu
from jax.sharding import PartitionSpec as P

UP, DOWN, SIDE, CORE = range(4)


def exchange_kernel(
    n, x_ref, f_ref, g_ref, gram_ref, slab_ref, cols_ref,
    xall, fv, gv, proj, proj_low, part, out0, in0, out1, in1, out2, in2, final,
    local_sem, x_recv, x_send, s_recv, s_send, c_recv, c_send,
    r_recv, r_send, z2_recv, z2_send, z3_recv, z3_send,
):
    me = lax.axis_index("row")
    depth = n // 4
    z, y, c = me // 4, (me // 2) % 2, me % 2
    sh = x_ref.shape[0]
    tokens = n * sh
    slab = slab_ref.shape[1]
    width = cols_ref.shape[1]
    feat = f_ref.shape[0]

    def index(zz, yy, cc):
        return zz * 4 + yy * 2 + cc

    side, peer = index(z, 1 - y, c), index(z, y, 1 - c)

    def rows(start, size):
        return pl.ds(pl.multiple_of(start, size), size)

    load_f = pltpu.make_async_copy(f_ref, fv, local_sem.at[0])
    load_x = pltpu.make_async_copy(x_ref, xall.at[rows(me * sh, sh), :], local_sem.at[1])
    load_g = pltpu.make_async_copy(g_ref, gv, local_sem.at[2])
    load_x.start()
    load_g.start()
    load_f.start()

    barrier = pltpu.get_barrier_semaphore()
    for k in range(1, n):
        pl.semaphore_signal(
            barrier, inc=1, device_id={"row": (me + k) % n}, device_id_type=pl.DeviceIdType.MESH
        )
    pl.semaphore_wait(barrier, n - 1)

    def send(src, dst, send_sem, recv_sem, target):
        return pltpu.make_async_remote_copy(
            src_ref=src, dst_ref=dst, send_sem=send_sem, recv_sem=recv_sem,
            device_id={"row": target}, device_id_type=pl.DeviceIdType.MESH,
        )

    chips = n // 2
    chip = z * 2 + y
    window = min(chips, chips // 2 + 1)
    union = min(chips, window + 1)

    class Gather:
        def __init__(self, buf, recv, sems, pieces):
            self.buf, self.recv, self.sems, self.pieces = buf, recv, sems, pieces
            self.width = buf.shape[1] // pieces
            self.near = window if pieces > 1 else 1
            self.end = union if pieces > 1 else 1

        def copy(self, origin, kind, target, first, count, src=None):
            cols = pl.ds(pl.multiple_of(first * self.width, self.width), count * self.width)
            view = self.buf.at[rows(origin * sh, sh), cols]
            return send(
                view if src is None else src.at[:, cols], view,
                self.sems.at[kind, origin], self.recv.at[origin], target,
            )

        def start(self, origin, kind, target, first, count, src=None):
            if self.pieces == 1:
                self.copy(origin, kind, target, 0, 1, src).start()
                return

            @pl.loop(0, count)
            def _(k):
                self.copy(origin, kind, target, (first + k) % self.pieces, 1, src).start()

        def along(self, origin, kind, src=None):
            to = z + 1 if kind == UP else z - 1
            last = (to == depth - 1) | (to == 0)
            count = jnp.where(last, self.end, self.pieces)
            self.start(origin, kind, index(to, y, c), to * 2, count, src)

        def near_by(self, origin, src=None):
            self.start(origin, SIDE, side, z * 2 + 1 - y, self.near, src)
            self.start(origin, CORE, peer, chip, self.near, src)

        def arrived(self, origin, count):
            self.copy(origin, CORE, peer, 0, count).wait_recv()

        def own(self, src):
            @pl.when(z + 1 < depth)
            def _():
                self.along(me, UP, src)

            @pl.when(z > 0)
            def _():
                self.along(me, DOWN, src)

            self.near_by(me, src)

        def column(self, k):
            def came(origin):
                last = (z == depth - 1) | (z == 0)

                @pl.when(last)
                def _():
                    self.arrived(origin, self.end)

                @pl.when(jnp.logical_not(last))
                def _():
                    self.arrived(origin, self.pieces)

            @pl.when(z - k >= 0)
            def _():
                origin = index(z - k, y, c)
                came(origin)

                @pl.when(z + 1 < depth)
                def _():
                    self.along(origin, UP)

                self.near_by(origin)

            @pl.when(z + k < depth)
            def _():
                origin = index(z + k, y, c)
                came(origin)

                @pl.when(z > 0)
                def _():
                    self.along(origin, DOWN)

                self.near_by(origin)

        def across(self, plane):
            origin = index(plane, 1 - y, c)
            self.arrived(origin, self.near)
            self.start(origin, CORE, peer, chip, self.near)

        def whole(self, plane):
            self.arrived(index(plane, 0, 1 - c), self.near)
            self.arrived(index(plane, 1, 1 - c), self.near)

        def drain(self):
            def sent(origin, kind, count):
                self.copy(origin, kind, peer, 0, count).wait_send()

            for plane in range(depth):
                origin = index(plane, y, c)
                for kind, edge, gate in (
                    (UP, z + 1 == depth - 1, (plane <= z) & (z + 1 < depth)),
                    (DOWN, z - 1 == 0, (plane >= z) & (z > 0)),
                ):
                    @pl.when(gate & edge)
                    def _():
                        sent(origin, kind, self.end)

                    @pl.when(gate & jnp.logical_not(edge))
                    def _():
                        sent(origin, kind, self.pieces)

                sent(origin, SIDE, self.near)
                sent(origin, CORE, self.near)
                sent(index(plane, 1 - y, c), CORE, self.near)

    gx = Gather(xall, x_recv, x_send, chips)
    gs = Gather(slab_ref, s_recv, s_send, 1)
    gx.own(x_ref)

    flip = z >= (depth + 1) // 2
    zm = jnp.where(flip, depth - 1 - z, z)

    def plane_at(t):
        near = zm - (t + 1) // 2 if t % 2 else zm + t // 2
        p = jnp.where(t <= 2 * zm, near, t)
        return jnp.where(flip, depth - 1 - p, p)

    block = 4 * sh
    tile = min(256, feat)

    def project(plane):
        xs = rows(plane * block, block)

        @pl.loop(0, feat // tile)
        def _(j):
            fs = rows(j * tile, tile)
            edge, inner = jnp.zeros((block, tile), jnp.float32), jnp.zeros((block, tile), jnp.float32)
            for k in range(window):
                cs = rows((chip + k) % chips * (2 * feat), 2 * feat)
                term = lax.dot_general(
                    xall[xs, cs], fv[fs, cs], (((1,), (1,)), ((), ())),
                    preferred_element_type=jnp.float32,
                )
                if k == 0 or 2 * k == chips:
                    edge = edge + term
                else:
                    inner = inner + term
            value = inner + 0.5 * edge
            high = value.astype(jnp.bfloat16)
            proj[xs, fs] = high
            proj_low[xs, fs] = (value - high.astype(jnp.float32)).astype(jnp.bfloat16)

    def cols_copy(d, origin):
        return send(
            gv.at[:, rows(d * width, width)],
            cols_ref.at[rows(origin * sh, sh), :],
            c_send.at[d], c_recv.at[origin], d,
        )

    load_x.wait()
    load_g.wait()
    load_f.wait()
    own_slab = pltpu.make_async_copy(
        gv.at[:, pl.ds(0, slab)], slab_ref.at[rows(me * sh, sh), :], local_sem.at[3]
    )
    own_cols = pltpu.make_async_copy(
        gv.at[:, rows(me * width, width)], cols_ref.at[rows(me * sh, sh), :], local_sem.at[4]
    )
    own_slab.start()
    own_cols.start()

    def send_cols(part, parts):
        for k in range(1, n):
            if k * parts // n == part:
                cols_copy((me + k * 5) % n if n % 5 else (me + k) % n, me).start()

    SLAB_AT = depth - 2
    COLS_AT = -1
    done = depth - 1 - SLAB_AT
    for t in range(depth):
        if t > 0:
            gx.column(t)
        if t == SLAB_AT:
            gs.own(gv.at[:, pl.ds(0, slab)])
        if t > SLAB_AT:
            gs.column(t - SLAB_AT)
        if t == COLS_AT:
            send_cols(0, 1)
        plane = plane_at(t)
        gx.across(plane)
        gx.whole(plane)
        project(plane)

    own_features = rows(me * feat, feat)
    half, quarter = tokens // 2, tokens // 4

    def partial_rows(start, size):
        some = rows(start, size)
        total = jnp.zeros((size, tokens), jnp.float32)
        for piece in (proj, proj_low):
            for left, right in ((piece[some, :], xall[:, own_features]), (xall[some, own_features], piece[...])):
                total = total + lax.dot_general(
                    left, right, (((1,), (1,)), ((), ())), preferred_element_type=jnp.float32
                )
        return total

    out0[...] = partial_rows((1 - c) * half, half)
    core_sum = send(out0, in0, r_send.at[0], r_recv.at[0], peer)
    core_sum.start()
    part[...] = partial_rows(c * half, half)
    if COLS_AT < 0:
        send_cols(0, 4)
    if done + 1 < depth:
        gs.column(done + 1)
    core_sum.wait_recv()
    gone, kept = rows((1 - y) * quarter, quarter), rows(y * quarter, quarter)
    out1[...] = (part[gone, :] + in0[gone, :]).astype(jnp.bfloat16)
    side_sum = send(out1, in1, r_send.at[1], r_recv.at[1], side)
    side_sum.start()
    part[kept, :] = part[kept, :] + in0[kept, :]
    if COLS_AT < 0:
        send_cols(1, 4)
    for k in range(done + 2, depth):
        gs.column(k)
    side_sum.wait_recv()
    part[kept, :] = part[kept, :] + in1[...].astype(jnp.float32)
    out2[...] = part[kept, :].astype(jnp.bfloat16)

    def z_sum(k):
        zz = (z + k) % depth
        return send(
            out2.at[rows(zz * sh, sh), :], in2.at[k], z2_send.at[k], z2_recv.at[k], index(zz, y, c)
        )

    for k in range(1, depth):
        z_sum(k).start()
    if COLS_AT < 0:
        send_cols(2, 4)
    for t in range(depth // 2):
        gs.across(plane_at(t))
    total = part[rows(y * quarter + z * sh, sh), :]
    for k in range(1, depth):
        z_sum(k).wait_recv()
        total = total + in2[k].astype(jnp.float32)
    scale = float(n * feat) ** (-0.5)
    base = c * half + y * quarter
    mine = rows(base + z * sh, sh)
    final[mine, :] = (total * scale).astype(jnp.bfloat16)

    def z_spread(k):
        zz = (z + k) % depth
        return send(
            final.at[mine, :], final.at[mine, :], z3_send.at[k], z3_recv.at[k], index(zz, y, c)
        )

    for k in range(1, depth):
        z_spread(k).start()
    if COLS_AT < 0:
        send_cols(3, 4)
    for t in range(depth // 2, depth):
        gs.across(plane_at(t))
    for k in range(1, depth):
        z_spread(k).wait_recv()
    view = final.at[rows(base, quarter), :]
    side_spread = send(view, view, r_send.at[2], r_recv.at[2], side)
    side_spread.start()
    side_spread.wait_recv()
    view = final.at[rows(c * half, half), :]
    core_spread = send(view, view, r_send.at[3], r_recv.at[3], peer)
    core_spread.start()
    core_spread.wait_recv()
    gram_ref[...] = final[...]
    for t in range(depth):
        gs.whole(plane_at(t))
    for k in range(1, n):
        cols_copy(me, (me + k) % n).wait_recv()

    gx.drain()
    gs.drain()
    for k in range(1, n):
        cols_copy((me + k) % n, me).wait_send()
    for copy in (core_sum, side_sum, side_spread, core_spread):
        copy.wait_send()
    for k in range(1, depth):
        z_sum(k).wait_send()
        z_spread(k).wait_send()
    own_slab.wait()
    own_cols.wait()


def exchange(n, x, f, g, slab):
    sh, din = x.shape
    feat = f.shape[0]
    tokens, depth = n * sh, n // 4
    width = g.shape[1] // n
    half, quarter = tokens // 2, tokens // 4
    bf, dma = jnp.bfloat16, pltpu.SemaphoreType.DMA
    anyspace = pl.BlockSpec(memory_space=pl.ANY)
    return pl.pallas_call(
        functools.partial(exchange_kernel, n),
        out_shape=(
            jax.ShapeDtypeStruct((tokens, tokens), bf),
            jax.ShapeDtypeStruct((tokens, slab), bf),
            jax.ShapeDtypeStruct((tokens, width), bf),
        ),
        in_specs=[anyspace] * 3,
        out_specs=(pl.BlockSpec(memory_space=pltpu.VMEM), anyspace, anyspace),
        scratch_shapes=[
            pltpu.VMEM((tokens, din), bf),
            pltpu.VMEM(f.shape, bf),
            pltpu.VMEM(g.shape, bf),
            pltpu.VMEM((tokens, feat), bf),
            pltpu.VMEM((tokens, feat), bf),
            pltpu.VMEM((half, tokens), jnp.float32),
            pltpu.VMEM((half, tokens), jnp.float32),
            pltpu.VMEM((half, tokens), jnp.float32),
            pltpu.VMEM((quarter, tokens), bf),
            pltpu.VMEM((quarter, tokens), bf),
            pltpu.VMEM((quarter, tokens), bf),
            pltpu.VMEM((depth, sh, tokens), bf),
            pltpu.VMEM((tokens, tokens), bf),
            dma((5,)), dma((n,)), dma((4, n)), dma((n,)), dma((4, n)),
            dma((n,)), dma((n,)), dma((4,)), dma((4,)),
            dma((depth,)), dma((depth,)), dma((depth,)), dma((depth,)),
        ],
        compiler_params=pltpu.CompilerParams(
            collective_id=0, has_side_effects=True, vmem_limit_bytes=60 * 1024 * 1024
        ),
    )(x, f, g)


def per_device(n, inputs, input_factor, out_grads, output_factor):
    slab_width = output_factor.shape[1]
    gram, slab_all, grad_cols = exchange(n, inputs, input_factor, out_grads, slab_width)
    left = lax.dot_general(
        grad_cols, gram, (((0,), (0,)), ((), ())), preferred_element_type=jnp.float32
    ).astype(jnp.bfloat16)
    update = jnp.dot(left, slab_all, preferred_element_type=jnp.float32)
    return output_factor + update * (1.0 / gram.shape[0])


def solution(mesh):
    spec = P(("groups", "row"), None)
    return jax.shard_map(
        functools.partial(per_device, mesh.shape["row"]),
        mesh=mesh, in_specs=(spec,) * 4, out_specs=spec, check_vma=False,
    )
```

```python
import functools

import jax
import jax.numpy as jnp
from jax import lax
from jax.experimental import pallas as pl
from jax.experimental.pallas import tpu as pltpu
from jax.sharding import PartitionSpec as P

UP, DOWN, SIDE, CORE = range(4)


def exchange_kernel(
    n, x_ref, f_ref, g_ref, gram_ref, slab_ref, cols_ref,
    xall, fv, gv, proj, proj_low, part, out0, in0, out1, in1, out2, in2, final,
    local_sem, x_recv, x_send, s_recv, s_send, c_recv, c_send,
    r_recv, r_send, z2_recv, z2_send, z3_recv, z3_send,
):
    me = lax.axis_index("row")
    depth = n // 4
    z, y, c = me // 4, (me // 2) % 2, me % 2
    sh = x_ref.shape[0]
    tokens = n * sh
    slab = slab_ref.shape[1]
    width = cols_ref.shape[1]
    feat = f_ref.shape[0]

    def index(zz, yy, cc):
        return zz * 4 + yy * 2 + cc

    side, peer = index(z, 1 - y, c), index(z, y, 1 - c)

    def rows(start, size):
        return pl.ds(pl.multiple_of(start, size), size)

    load_f = pltpu.make_async_copy(f_ref, fv, local_sem.at[0])
    load_x = pltpu.make_async_copy(x_ref, xall.at[rows(me * sh, sh), :], local_sem.at[1])
    load_g = pltpu.make_async_copy(g_ref, gv, local_sem.at[2])
    load_x.start()
    load_g.start()
    load_f.start()

    barrier = pltpu.get_barrier_semaphore()
    for k in range(1, n):
        pl.semaphore_signal(
            barrier, inc=1, device_id={"row": (me + k) % n}, device_id_type=pl.DeviceIdType.MESH
        )
    pl.semaphore_wait(barrier, n - 1)

    def send(src, dst, send_sem, recv_sem, target):
        return pltpu.make_async_remote_copy(
            src_ref=src, dst_ref=dst, send_sem=send_sem, recv_sem=recv_sem,
            device_id={"row": target}, device_id_type=pl.DeviceIdType.MESH,
        )

    chips = n // 2
    chip = z * 2 + y
    window = min(chips, chips // 2 + 1)
    union = min(chips, window + 1)

    class Gather:
        def __init__(self, buf, recv, sems, pieces):
            self.buf, self.recv, self.sems, self.pieces = buf, recv, sems, pieces
            self.width = buf.shape[1] // pieces
            self.near = window if pieces > 1 else 1
            self.end = union if pieces > 1 else 1

        def copy(self, origin, kind, target, first, count, src=None):
            cols = pl.ds(pl.multiple_of(first * self.width, self.width), count * self.width)
            view = self.buf.at[rows(origin * sh, sh), cols]
            return send(
                view if src is None else src.at[:, cols], view,
                self.sems.at[kind, origin], self.recv.at[origin], target,
            )

        def start(self, origin, kind, target, first, count, src=None):
            if self.pieces == 1:
                self.copy(origin, kind, target, 0, 1, src).start()
                return

            @pl.loop(0, count)
            def _(k):
                self.copy(origin, kind, target, (first + k) % self.pieces, 1, src).start()

        def along(self, origin, kind, src=None):
            to = z + 1 if kind == UP else z - 1
            last = (to == depth - 1) | (to == 0)
            count = jnp.where(last, self.end, self.pieces)
            self.start(origin, kind, index(to, y, c), to * 2, count, src)

        def near_by(self, origin, src=None):
            self.start(origin, SIDE, side, z * 2 + 1 - y, self.near, src)
            self.start(origin, CORE, peer, chip, self.near, src)

        def arrived(self, origin, count):
            self.copy(origin, CORE, peer, 0, count).wait_recv()

        def own(self, src):
            @pl.when(z + 1 < depth)
            def _():
                self.along(me, UP, src)

            @pl.when(z > 0)
            def _():
                self.along(me, DOWN, src)

            self.near_by(me, src)

        def column(self, k):
            def came(origin):
                last = (z == depth - 1) | (z == 0)

                @pl.when(last)
                def _():
                    self.arrived(origin, self.end)

                @pl.when(jnp.logical_not(last))
                def _():
                    self.arrived(origin, self.pieces)

            @pl.when(z - k >= 0)
            def _():
                origin = index(z - k, y, c)
                came(origin)

                @pl.when(z + 1 < depth)
                def _():
                    self.along(origin, UP)

                self.near_by(origin)

            @pl.when(z + k < depth)
            def _():
                origin = index(z + k, y, c)
                came(origin)

                @pl.when(z > 0)
                def _():
                    self.along(origin, DOWN)

                self.near_by(origin)

        def across(self, plane):
            origin = index(plane, 1 - y, c)
            self.arrived(origin, self.near)
            self.start(origin, CORE, peer, chip, self.near)

        def whole(self, plane):
            self.arrived(index(plane, 0, 1 - c), self.near)
            self.arrived(index(plane, 1, 1 - c), self.near)

        def drain(self):
            def sent(origin, kind, count):
                self.copy(origin, kind, peer, 0, count).wait_send()

            for plane in range(depth):
                origin = index(plane, y, c)
                for kind, edge, gate in (
                    (UP, z + 1 == depth - 1, (plane <= z) & (z + 1 < depth)),
                    (DOWN, z - 1 == 0, (plane >= z) & (z > 0)),
                ):
                    @pl.when(gate & edge)
                    def _():
                        sent(origin, kind, self.end)

                    @pl.when(gate & jnp.logical_not(edge))
                    def _():
                        sent(origin, kind, self.pieces)

                sent(origin, SIDE, self.near)
                sent(origin, CORE, self.near)
                sent(index(plane, 1 - y, c), CORE, self.near)

    gx = Gather(xall, x_recv, x_send, chips)
    gs = Gather(slab_ref, s_recv, s_send, 1)
    gx.own(x_ref)

    flip = z >= (depth + 1) // 2
    zm = jnp.where(flip, depth - 1 - z, z)

    def plane_at(t):
        near = zm - (t + 1) // 2 if t % 2 else zm + t // 2
        p = jnp.where(t <= 2 * zm, near, t)
        return jnp.where(flip, depth - 1 - p, p)

    block = 4 * sh
    tile = min(256, feat)

    def project(plane):
        xs = rows(plane * block, block)

        @pl.loop(0, feat // tile)
        def _(j):
            fs = rows(j * tile, tile)
            edge, inner = jnp.zeros((block, tile), jnp.float32), jnp.zeros((block, tile), jnp.float32)
            for k in range(window):
                cs = rows((chip + k) % chips * (2 * feat), 2 * feat)
                term = lax.dot_general(
                    xall[xs, cs], fv[fs, cs], (((1,), (1,)), ((), ())),
                    preferred_element_type=jnp.float32,
                )
                if k == 0 or 2 * k == chips:
                    edge = edge + term
                else:
                    inner = inner + term
            value = inner + 0.5 * edge
            high = value.astype(jnp.bfloat16)
            proj[xs, fs] = high
            proj_low[xs, fs] = (value - high.astype(jnp.float32)).astype(jnp.bfloat16)

    def cols_copy(d, origin):
        return send(
            gv.at[:, rows(d * width, width)],
            cols_ref.at[rows(origin * sh, sh), :],
            c_send.at[d], c_recv.at[origin], d,
        )

    load_x.wait()
    load_g.wait()
    load_f.wait()
    own_slab = pltpu.make_async_copy(
        gv.at[:, pl.ds(0, slab)], slab_ref.at[rows(me * sh, sh), :], local_sem.at[3]
    )
    own_cols = pltpu.make_async_copy(
        gv.at[:, rows(me * width, width)], cols_ref.at[rows(me * sh, sh), :], local_sem.at[4]
    )
    own_slab.start()
    own_cols.start()

    def send_cols(part, parts):
        for k in range(1, n):
            if k * parts // n == part:
                cols_copy((me + k * 5) % n if n % 5 else (me + k) % n, me).start()

    SLAB_AT = depth - 2
    COLS_AT = depth - 1
    done = depth - 1 - SLAB_AT
    for t in range(depth):
        if t > 0:
            gx.column(t)
        if t == SLAB_AT:
            gs.own(gv.at[:, pl.ds(0, slab)])
        if t > SLAB_AT:
            gs.column(t - SLAB_AT)
        if t == COLS_AT:
            send_cols(0, 1)
        plane = plane_at(t)
        gx.across(plane)
        gx.whole(plane)
        project(plane)

    own_features = rows(me * feat, feat)
    half, quarter = tokens // 2, tokens // 4

    def partial_rows(start, size):
        some = rows(start, size)
        total = jnp.zeros((size, tokens), jnp.float32)
        for piece in (proj, proj_low):
            for left, right in ((piece[some, :], xall[:, own_features]), (xall[some, own_features], piece[...])):
                total = total + lax.dot_general(
                    left, right, (((1,), (1,)), ((), ())), preferred_element_type=jnp.float32
                )
        return total

    out0[...] = partial_rows((1 - c) * half, half)
    core_sum = send(out0, in0, r_send.at[0], r_recv.at[0], peer)
    core_sum.start()
    part[...] = partial_rows(c * half, half)
    if COLS_AT < 0:
        send_cols(0, 4)
    if done + 1 < depth:
        gs.column(done + 1)
    core_sum.wait_recv()
    gone, kept = rows((1 - y) * quarter, quarter), rows(y * quarter, quarter)
    out1[...] = (part[gone, :] + in0[gone, :]).astype(jnp.bfloat16)
    side_sum = send(out1, in1, r_send.at[1], r_recv.at[1], side)
    side_sum.start()
    part[kept, :] = part[kept, :] + in0[kept, :]
    if COLS_AT < 0:
        send_cols(1, 4)
    for k in range(done + 2, depth):
        gs.column(k)
    side_sum.wait_recv()
    part[kept, :] = part[kept, :] + in1[...].astype(jnp.float32)
    out2[...] = part[kept, :].astype(jnp.bfloat16)

    def z_sum(k):
        zz = (z + k) % depth
        return send(
            out2.at[rows(zz * sh, sh), :], in2.at[k], z2_send.at[k], z2_recv.at[k], index(zz, y, c)
        )

    for k in range(1, depth):
        z_sum(k).start()
    if COLS_AT < 0:
        send_cols(2, 4)
    for t in range(depth // 2):
        gs.across(plane_at(t))
    total = part[rows(y * quarter + z * sh, sh), :]
    for k in range(1, depth):
        z_sum(k).wait_recv()
        total = total + in2[k].astype(jnp.float32)
    scale = float(n * feat) ** (-0.5)
    base = c * half + y * quarter
    mine = rows(base + z * sh, sh)
    final[mine, :] = (total * scale).astype(jnp.bfloat16)

    def z_spread(k):
        zz = (z + k) % depth
        return send(
            final.at[mine, :], final.at[mine, :], z3_send.at[k], z3_recv.at[k], index(zz, y, c)
        )

    for k in range(1, depth):
        z_spread(k).start()
    if COLS_AT < 0:
        send_cols(3, 4)
    for t in range(depth // 2, depth):
        gs.across(plane_at(t))
    for k in range(1, depth):
        z_spread(k).wait_recv()
    view = final.at[rows(base, quarter), :]
    side_spread = send(view, view, r_send.at[2], r_recv.at[2], side)
    side_spread.start()
    side_spread.wait_recv()
    view = final.at[rows(c * half, half), :]
    core_spread = send(view, view, r_send.at[3], r_recv.at[3], peer)
    core_spread.start()
    core_spread.wait_recv()
    gram_ref[...] = final[...]
    for t in range(depth):
        gs.whole(plane_at(t))
    for k in range(1, n):
        cols_copy(me, (me + k) % n).wait_recv()

    gx.drain()
    gs.drain()
    for k in range(1, n):
        cols_copy((me + k) % n, me).wait_send()
    for copy in (core_sum, side_sum, side_spread, core_spread):
        copy.wait_send()
    for k in range(1, depth):
        z_sum(k).wait_send()
        z_spread(k).wait_send()
    own_slab.wait()
    own_cols.wait()


def exchange(n, x, f, g, slab):
    sh, din = x.shape
    feat = f.shape[0]
    tokens, depth = n * sh, n // 4
    width = g.shape[1] // n
    half, quarter = tokens // 2, tokens // 4
    bf, dma = jnp.bfloat16, pltpu.SemaphoreType.DMA
    anyspace = pl.BlockSpec(memory_space=pl.ANY)
    return pl.pallas_call(
        functools.partial(exchange_kernel, n),
        out_shape=(
            jax.ShapeDtypeStruct((tokens, tokens), bf),
            jax.ShapeDtypeStruct((tokens, slab), bf),
            jax.ShapeDtypeStruct((tokens, width), bf),
        ),
        in_specs=[anyspace] * 3,
        out_specs=(pl.BlockSpec(memory_space=pltpu.VMEM), anyspace, anyspace),
        scratch_shapes=[
            pltpu.VMEM((tokens, din), bf),
            pltpu.VMEM(f.shape, bf),
            pltpu.VMEM(g.shape, bf),
            pltpu.VMEM((tokens, feat), bf),
            pltpu.VMEM((tokens, feat), bf),
            pltpu.VMEM((half, tokens), jnp.float32),
            pltpu.VMEM((half, tokens), jnp.float32),
            pltpu.VMEM((half, tokens), jnp.float32),
            pltpu.VMEM((quarter, tokens), bf),
            pltpu.VMEM((quarter, tokens), bf),
            pltpu.VMEM((quarter, tokens), bf),
            pltpu.VMEM((depth, sh, tokens), bf),
            pltpu.VMEM((tokens, tokens), bf),
            dma((5,)), dma((n,)), dma((4, n)), dma((n,)), dma((4, n)),
            dma((n,)), dma((n,)), dma((4,)), dma((4,)),
            dma((depth,)), dma((depth,)), dma((depth,)), dma((depth,)),
        ],
        compiler_params=pltpu.CompilerParams(
            collective_id=0, has_side_effects=True, vmem_limit_bytes=60 * 1024 * 1024
        ),
    )(x, f, g)


def per_device(n, inputs, input_factor, out_grads, output_factor):
    slab_width = output_factor.shape[1]
    gram, slab_all, grad_cols = exchange(n, inputs, input_factor, out_grads, slab_width)
    left = lax.dot_general(
        grad_cols, gram, (((0,), (0,)), ((), ())), preferred_element_type=jnp.float32
    ).astype(jnp.bfloat16)
    update = jnp.dot(left, slab_all, preferred_element_type=jnp.float32)
    return output_factor + update * (1.0 / gram.shape[0])


def solution(mesh):
    spec = P(("groups", "row"), None)
    return jax.shard_map(
        functools.partial(per_device, mesh.shape["row"]),
        mesh=mesh, in_specs=(spec,) * 4, out_specs=spec, check_vma=False,
    )
```
